32 devices in a mesh: dp: 4 (over y, core), seq: 8 (over z, x).
Axes of the slice: x: 2, y: 2, z: 4, core: 2. Of those that a mesh axis runs over, the one named last changes fastest.
Arguments:
- query: bfloat16 [8, 2048, 32, 128], P('dp', 'seq'), may hold values from -128 to 128
- keys: bfloat16 [8, 2048, 4, 128], P('dp', 'seq'), may hold values from -4.5 to 4.5
- values: bfloat16 [8, 2048, 4, 128], P('dp', 'seq'), may hold values from -6 to 6
- output: bfloat16 [8, 2048, 32, 128], P('dp', 'seq'), may hold values from -6 to 6
- out_grad: bfloat16 [8, 2048, 32, 128], P('dp', 'seq'), may hold values from -6 to 6
- lengths: int32 [8], P('dp'), may hold values from 341 to 2048, as said below
- margins: float32 [4], P('dp'), may hold values from -3 to 3
Outputs:
- query_grad: bfloat16 [8, 2048, 32, 128], P('dp', 'seq')
- key_grad: bfloat16 [8, 2048, 4, 128], P('dp', 'seq')
- value_grad: bfloat16 [8, 2048, 4, 128], P('dp', 'seq')
The draws below stay inside these ranges and needn't reach their ends.
Inputs may be any that keep to these rules, and one draw needn't show every extreme that they name: `lengths`: sequence 2p is pair p's chosen response and 2p + 1 its rejected one; some sequence has exactly 2048 tokens.
All inputs are finite; a program needn't handle non-finite values.
Results may differ from the reference program's by a relative error of at most 0.009.
Values may be sent and summed in bfloat16 or wider, within the bound.
A program may use at most 128 MiB of HBM per device.

```python
import math
import jax
import jax.numpy as jnp
from jax import lax

HEADS = 32
KV_HEADS = 4
HEAD_DIM = 128
MAX_LEN = 2048
PAIRS_DEV = 1
PAIRS = 4
SEQS = 8
N_DP = 4


def key_base(key):
    base = jax.random.normal(jax.random.fold_in(key, 11), (SEQS, MAX_LEN, KV_HEADS, HEAD_DIM), jnp.float32)
    return jnp.clip(base, -4.5, 4.5)


def draw_keys(key, part):
    base = key_base(key)
    return base.astype(jnp.bfloat16)


def draw_query(key, part):
    fresh = jax.random.normal(jax.random.fold_in(key, 12), (SEQS, MAX_LEN, HEADS, HEAD_DIM), jnp.float32)
    fresh = jnp.clip(fresh, -4.5, 4.5)
    return fresh.astype(jnp.bfloat16)


def draw_lengths(key, part):
    index = jnp.arange(SEQS)
    group = index // (2 * PAIRS_DEV)
    third = MAX_LEN // 3
    upper = third + (MAX_LEN - third) * group // max(N_DP - 1, 1)
    lower = upper // 2
    raw = jax.random.randint(key, (SEQS,), 0, 1048576)
    length = lower + raw % (upper - lower + 1)
    length = jnp.where(index == (N_DP - 1) * 2 * PAIRS_DEV, MAX_LEN, length)
    length = jnp.where(index == 2 * PAIRS_DEV - 1, third // 2, length)
    return length.astype(jnp.int32)


def block_levels(rng, shape, shards, smallest, top_value):
    factor_of, own = 1.0, jax.random.fold_in(rng, 6)
    for dim, blocks in shards:
        steps = jnp.exp(jax.random.uniform(jax.random.fold_in(own, dim), (blocks,), jnp.float32, smallest / len(shards), top_value / len(shards)))
        factor_of = factor_of * jnp.repeat(steps, shape[dim] // blocks).reshape([-1 if axis == dim else 1 for axis in range(len(shape))])
    return factor_of


def bell_draw(own_key, dims, scale, limit, cuts=(), dtype=jnp.bfloat16):
    drawn = scale * jax.random.normal(own_key, dims, jnp.float32)
    if cuts:
        drawn = drawn * block_levels(own_key, dims, cuts, -0.22, 0.18)
    return jnp.clip(drawn, -limit, limit).astype(dtype)


def setup_inputs(seed: int = 0) -> dict:
    key_of = jax.random.split(jax.random.key(seed), 8)
    query = draw_query(jax.random.fold_in(key_of[7], 71), 0)
    keys = draw_keys(jax.random.fold_in(key_of[7], 71), 0)
    values = bell_draw(key_of[2], (SEQS, MAX_LEN, KV_HEADS, HEAD_DIM), 1.0, 6.0, ((0, 4), (1, 8)))
    output = bell_draw(key_of[3], (SEQS, MAX_LEN, HEADS, HEAD_DIM), 1.0, 6.0, ((0, 4), (1, 8)))
    out_grad = bell_draw(key_of[4], (SEQS, MAX_LEN, HEADS, HEAD_DIM), 1.0, 6.0, ((0, 4), (1, 8)))
    lengths = draw_lengths(jax.random.fold_in(key_of[7], 71), 0)
    margins = jnp.clip(jax.random.uniform(key_of[6], (PAIRS,), jnp.float32, -3.0, 3.0) * block_levels(key_of[6], (PAIRS,), ((0, 4),), -0.4, 0.0), -3.0, 3.0)
    return dict(query=query, keys=keys, values=values, output=output, out_grad=out_grad, lengths=lengths, margins=margins)


def sequence_grads(query, scaled, keys, values, delta):
    full_len, heads, head_dim = query.shape
    slots = keys.shape[1]
    repeat = heads // slots
    block = min(512, full_len)
    scale = 1.0 / math.sqrt(head_dim)
    q_four = query.reshape(full_len, slots, repeat, head_dim).astype(jnp.float32)
    g_four = scaled.reshape(full_len, slots, repeat, head_dim).astype(jnp.float32)
    d_three = delta.reshape(full_len, slots, repeat)
    keys_wide = keys.astype(jnp.float32)
    values_wide = values.astype(jnp.float32)
    key_pos = jnp.arange(full_len)
    key_acc = jnp.zeros((full_len, slots, head_dim), jnp.float32)
    value_acc = jnp.zeros((full_len, slots, head_dim), jnp.float32)
    pieces = []
    for index in range(full_len // block):
        start = index * block
        q_block = q_four[start:start + block]
        g_block = g_four[start:start + block]
        d_block = jnp.transpose(d_three[start:start + block], (1, 2, 0))[..., None]
        scores = jnp.einsum('isrd,jsd->srij', q_block, keys_wide) * scale
        query_pos = start + jnp.arange(block)
        causal = key_pos[None, :] <= query_pos[:, None]
        scores = jnp.where(causal, scores, -jnp.inf)
        top = lax.optimization_barrier(jnp.max(scores, axis=-1, keepdims=True))
        lse = top + jnp.log(lax.optimization_barrier(jnp.sum(jnp.exp(scores - top), axis=-1, keepdims=True)))
        prob = jnp.exp(scores - lse)
        prob_low = lax.optimization_barrier(prob.astype(jnp.bfloat16)).astype(jnp.float32)
        value_acc = value_acc + jnp.einsum('srij,isrd->jsd', prob_low, g_block)
        dprob = jnp.einsum('isrd,jsd->srij', g_block, values_wide)
        dscore = prob * (dprob - d_block)
        dscore_low = lax.optimization_barrier(dscore.astype(jnp.bfloat16)).astype(jnp.float32)
        query_part = jnp.einsum('srij,jsd->isrd', dscore_low, keys_wide) * scale
        pieces.append(query_part.reshape(block, heads, head_dim).astype(jnp.bfloat16))
        key_acc = key_acc + jnp.einsum('srij,isrd->jsd', dscore_low, q_block)
    query_grad = jnp.concatenate(pieces, axis=0)
    return (query_grad, (key_acc * scale).astype(jnp.bfloat16), value_acc.astype(jnp.bfloat16))

def reference(query, keys, values, output, out_grad, lengths, margins):
    seqs = query.shape[0]
    total = jnp.sum(lengths)
    mean_len = total.astype(jnp.float32) / seqs
    weight = jax.nn.sigmoid(-margins)
    signs = jnp.tile(jnp.array([-1.0, 1.0], jnp.float32), margins.shape[0])
    coef = jnp.repeat(weight, 2) * signs * 4.0 * mean_len / lengths.astype(jnp.float32)
    live = (jnp.arange(MAX_LEN).astype(jnp.int32)[None, :] < lengths[:, None]).astype(jnp.float32)
    factor = coef[:, None] * live
    scaled = (out_grad.astype(jnp.float32) * factor[:, :, None, None]).astype(jnp.bfloat16)
    delta = lax.optimization_barrier(jnp.sum(scaled.astype(jnp.float32) * output.astype(jnp.float32), axis=3))
    query_grad, key_grad, value_grad = lax.map(lambda items: sequence_grads(*items), (query, scaled, keys, values, delta))
    return (query_grad, key_grad, value_grad)
```

```python
import functools
import math

import jax
import jax.numpy as jnp
from jax import lax
from jax.experimental import pallas as pl
from jax.experimental.pallas import tpu as pltpu
from jax.sharding import PartitionSpec as P

CHUNK_TOKENS = 64
LOW = -1e30


def attend_kernel(
    info,
    coef,
    query_ref,
    grad_ref,
    output_ref,
    kv_ref,
    *rest,
    scale,
    seq,
    chunk_tokens,
):
    query_grad_ref, kv_grad_ref, e_ref, m_ref, key_acc, value_acc, wide_ref = rest[-7:]
    toks, group, dim = query_ref.shape[1:]
    places = kv_ref.shape[0]
    rows = chunk_tokens * group
    place = info[0]
    length = info[1 + seq]
    factor_live = coef[seq]
    base = place * toks
    log2e = scale * math.log2(math.e)

    lane = lax.broadcasted_iota(jnp.int32, (toks, dim), 1)
    ones = jnp.where(lane < 3, 1.0, 0.0).astype(jnp.bfloat16)

    def zero_rest(j, _):
        kv_grad_ref[j] = jnp.zeros(kv_grad_ref.shape[1:], kv_grad_ref.dtype)
        return 0

    def prepare(j, _):
        key_acc[j] = jnp.zeros((toks, dim), jnp.float32)
        value_acc[j] = jnp.zeros((toks, dim), jnp.float32)
        wide_ref[j, :, :dim] = kv_ref[j, 0, 0, 1]
        wide_ref[j, :, dim:] = ones
        return 0

    lax.fori_loop(0, place + 1, prepare, 0)

    def chunk(c, _):
        tok0 = pl.multiple_of(c * chunk_tokens, chunk_tokens)
        here = pl.ds(tok0, chunk_tokens)

        @pl.when(base + tok0 >= length)
        def _():
            query_grad_ref[0, here] = jnp.zeros((chunk_tokens, group, dim), query_grad_ref.dtype)

        @pl.when(base + tok0 < length)
        def _():
            q = (
                query_ref[0, here].astype(jnp.float32).reshape(rows, dim).astype(jnp.bfloat16)
            )
            position = (
                base + tok0 + lax.broadcasted_iota(jnp.int32, (chunk_tokens, group, dim), 0)
            )
            factor = jnp.where(position < length, factor_live, 0.0)
            g = (grad_ref[0, here].astype(jnp.float32) * factor).reshape(rows, dim)
            g_low = g.astype(jnp.bfloat16)
            o = output_ref[0, here].astype(jnp.float32).reshape(rows, dim)
            delta = jnp.sum(g_low.astype(jnp.float32) * o, axis=-1, keepdims=True)
            high = delta.astype(jnp.bfloat16).astype(jnp.float32)
            middle = (delta - high).astype(jnp.bfloat16).astype(jnp.float32)
            low = delta - high - middle
            row_lane = lax.broadcasted_iota(jnp.int32, (rows, dim), 1)
            extra = jnp.where(
                row_lane == 0,
                -high,
                jnp.where(row_lane == 1, -middle, jnp.where(row_lane == 2, -low, 0.0)),
            ).astype(jnp.bfloat16)
            g_wide = jnp.concatenate([g_low, extra], axis=1)

            def scores_of(j):
                return lax.dot_general(
                    kv_ref[j, 0, 0, 0],
                    q,
                    (((1,), (1,)), ((), ())),
                    preferred_element_type=jnp.float32,
                )

            def absorb(j, s, carry):
                top, total = carry
                new = jnp.maximum(top, jnp.max(s, axis=0, keepdims=True) * log2e)
                e = jnp.exp2(s * log2e - new)
                e_ref[j] = e
                m_ref[j] = new
                total = total * jnp.exp2(top - new) + jnp.sum(e, axis=0, keepdims=True)
                return (new, total)

            carry = (jnp.full((1, rows), LOW, jnp.float32), jnp.zeros((1, rows), jnp.float32))
            carry = lax.fori_loop(0, place, lambda j, x: absorb(j, scores_of(j), x), carry)
            key_pos = lax.broadcasted_iota(jnp.int32, (toks, rows), 0)
            row_pos = tok0 + lax.broadcasted_iota(jnp.int32, (toks, rows), 1) // group
            top, total = absorb(
                place, jnp.where(key_pos <= row_pos, scores_of(place), LOW), carry
            )
            inverse = 1.0 / total

            def back(j, acc):
                prob = e_ref[j] * (jnp.exp2(m_ref[j] - top) * inverse)
                value_acc[j] += jnp.dot(
                    prob.astype(jnp.bfloat16), g_low, preferred_element_type=jnp.float32
                )
                dprob = lax.dot_general(
                    wide_ref[j],
                    g_wide,
                    (((1,), (1,)), ((), ())),
                    preferred_element_type=jnp.float32,
                )
                dscore = (prob * dprob).astype(jnp.bfloat16)
                key_acc[j] += jnp.dot(dscore, q, preferred_element_type=jnp.float32)
                return acc + lax.dot_general(
                    dscore,
                    kv_ref[j, 0, 0, 0],
                    (((0,), (0,)), ((), ())),
                    preferred_element_type=jnp.float32,
                )

            acc = lax.fori_loop(0, place + 1, back, jnp.zeros((rows, dim), jnp.float32))
            query_grad_ref[0, here] = (
                (acc * scale).reshape(chunk_tokens, group, dim).astype(query_grad_ref.dtype)
            )

        return 0

    lax.fori_loop(0, toks // chunk_tokens, chunk, 0)

    def finish(j, _):
        kv_grad_ref[j, 0, 0] = (key_acc[j] * scale).astype(kv_grad_ref.dtype)
        kv_grad_ref[j, 0, 1] = value_acc[j].astype(kv_grad_ref.dtype)
        return 0

    lax.fori_loop(0, place + 1, finish, 0)
    lax.fori_loop(place + 1, places, zero_rest, 0)


def attend(info, coef, query, grad, output, kv, seq, first, carry):
    seqs, toks, heads, dim = query.shape
    places, _, count = kv.shape[:3]
    kv_all = carry[1]
    group = heads // kv_all
    chunk_tokens = min(CHUNK_TOKENS, toks)
    rows = chunk_tokens * group
    token_spec = pl.BlockSpec((1, toks, group, dim), lambda h, *_: (seq, 0, first + h, 0))
    kv_spec = pl.BlockSpec((places, 1, 1, 2, toks, dim), lambda h, *_: (0, 0, h, 0, 0, 0))
    grad_spec = pl.BlockSpec((places, 1, 2, toks, dim), lambda h, *_: (0, h, 0, 0, 0))
    operands = [info, coef, query, grad, output, kv]
    in_specs = [token_spec, token_spec, token_spec, kv_spec]
    aliases = {}
    if carry[0] is not None:
        aliases = {len(operands): 0}
        operands.append(carry[0])
        in_specs.append(pl.BlockSpec(memory_space=pl.ANY))
    flops = 5 * 2 * heads // kv_all * count * toks * toks * places * dim
    return pl.pallas_call(
        functools.partial(
            attend_kernel,
            scale=1.0 / math.sqrt(dim),
            seq=seq,
            chunk_tokens=chunk_tokens,
        ),
        out_shape=(
            jax.ShapeDtypeStruct(query.shape, query.dtype),
            jax.ShapeDtypeStruct((places, count, 2, toks, dim), jnp.bfloat16),
        ),
        grid_spec=pltpu.PrefetchScalarGridSpec(
            num_scalar_prefetch=2,
            grid=(count,),
            in_specs=in_specs,
            out_specs=(token_spec, grad_spec),
            scratch_shapes=[
                pltpu.VMEM((places, toks, rows), jnp.float32),
                pltpu.VMEM((places, 1, rows), jnp.float32),
                pltpu.VMEM((places, toks, dim), jnp.float32),
                pltpu.VMEM((places, toks, dim), jnp.float32),
                pltpu.VMEM((places, toks, 2 * dim), jnp.bfloat16),
            ],
        ),
        input_output_aliases=aliases,
        cost_estimate=pl.CostEstimate(
            flops=flops,
            bytes_accessed=4 * 2 * toks * group * count * dim * 2,
            transcendentals=0,
        ),
        compiler_params=pltpu.CompilerParams(vmem_limit_bytes=48 * 1024 * 1024),
    )(*operands)


def body(query, keys, values, output, out_grad, lengths, margins):
    place = lax.axis_index("seq")
    seqs, toks, heads, dim = query.shape
    kv_heads = keys.shape[2]
    kv = jnp.stack([keys, values], axis=1).transpose(0, 3, 1, 2, 4)
    split = 1
    step = kv_heads // split
    gathered = {
        (s, c): lax.all_gather(kv[s : s + 1, c : c + step], "seq", axis=0, tiled=False)
        for s in range(seqs)
        for c in range(0, kv_heads, step)
    }
    total = lax.psum(jnp.sum(lengths), "dp")
    mean_len = total.astype(jnp.float32) / (seqs * lax.axis_size("dp"))
    weight = jax.nn.sigmoid(-margins)
    signs = jnp.tile(jnp.array([-1.0, 1.0], jnp.float32), margins.shape[0])
    coef = jnp.repeat(weight, 2) * signs * 4.0 * mean_len / lengths.astype(jnp.float32)
    info = jnp.concatenate([place[None].astype(jnp.int32), lengths.astype(jnp.int32)])
    query_grad = None
    parts = []
    for s in range(seqs):
        row = []
        for c in range(0, kv_heads, step):
            query_grad, kv_grad = attend(
                info, coef, query, out_grad, output, gathered[s, c], s, c, (query_grad, kv_heads)
            )
            row.append(lax.psum_scatter(kv_grad, "seq", scatter_dimension=0, tiled=False))
        parts.append(jnp.concatenate(row, axis=0) if split > 1 else row[0])
    grads = jnp.stack(parts)
    key_grad = grads[:, :, 0].transpose(0, 2, 1, 3)
    value_grad = grads[:, :, 1].transpose(0, 2, 1, 3)
    return (query_grad, key_grad, value_grad)


def solution(mesh):
    tokens = P("dp", "seq", None, None)
    return jax.shard_map(
        body,
        mesh=mesh,
        in_specs=(tokens,) * 5 + (P("dp"), P("dp")),
        out_specs=(tokens,) * 3,
        check_vma=False,
    )
```

```python
import functools
import math

import jax
import jax.numpy as jnp
from jax import lax
from jax.experimental import pallas as pl
from jax.experimental.pallas import tpu as pltpu
from jax.sharding import PartitionSpec as P

CHUNK_TOKENS = 64
SPLIT = 2
LOW = -1e30


def attend_kernel(
    info,
    coef,
    query_ref,
    grad_ref,
    output_ref,
    *rest,
    slots,
    scale,
    seq,
    chunk_tokens,
):
    kv_refs = rest[:slots]
    query_grad_ref, kv_grad_ref, e_ref, m_ref, key_acc, value_acc, keys_ref, wide_ref = rest[-8:]
    toks, group, dim = query_ref.shape[1:]
    rows = chunk_tokens * group
    place = info[0]
    side = info[1]
    length = info[2 + seq]
    factor_live = coef[seq]
    base = place * toks
    first, last = 2 - side, place - side + 2
    log2e = scale * math.log2(math.e)

    lane = lax.broadcasted_iota(jnp.int32, (toks, dim), 1)
    ones = jnp.where(lane < 3, 1.0, 0.0).astype(jnp.bfloat16)

    for j in range(slots):
        key_acc[j] = jnp.zeros((toks, dim), jnp.float32)
        value_acc[j] = jnp.zeros((toks, dim), jnp.float32)
        keys_ref[j] = kv_refs[j][0, 0]
        wide_ref[j, :, :dim] = kv_refs[j][0, 1]
        wide_ref[j, :, dim:] = ones

    def chunk(c, _):
        tok0 = pl.multiple_of(c * chunk_tokens, chunk_tokens)
        here = pl.ds(tok0, chunk_tokens)

        @pl.when(base + tok0 >= length)
        def _():
            query_grad_ref[0, here] = jnp.zeros((chunk_tokens, group, dim), query_grad_ref.dtype)

        @pl.when(base + tok0 < length)
        def _():
            q = (
                query_ref[0, here].astype(jnp.float32).reshape(rows, dim).astype(jnp.bfloat16)
            )
            position = (
                base + tok0 + lax.broadcasted_iota(jnp.int32, (chunk_tokens, group, dim), 0)
            )
            factor = jnp.where(position < length, factor_live, 0.0)
            g = (grad_ref[0, here].astype(jnp.float32) * factor).reshape(rows, dim)
            g_low = g.astype(jnp.bfloat16)
            o = output_ref[0, here].astype(jnp.float32).reshape(rows, dim)
            delta = jnp.sum(g_low.astype(jnp.float32) * o, axis=-1, keepdims=True)
            high = delta.astype(jnp.bfloat16).astype(jnp.float32)
            middle = (delta - high).astype(jnp.bfloat16).astype(jnp.float32)
            low = delta - high - middle
            row_lane = lax.broadcasted_iota(jnp.int32, (rows, dim), 1)
            extra = jnp.where(
                row_lane == 0,
                -high,
                jnp.where(row_lane == 1, -middle, jnp.where(row_lane == 2, -low, 0.0)),
            ).astype(jnp.bfloat16)
            g_wide = jnp.concatenate([g_low, extra], axis=1)

            def scores_of(j):
                return lax.dot_general(
                    keys_ref[j],
                    q,
                    (((1,), (1,)), ((), ())),
                    preferred_element_type=jnp.float32,
                )

            def absorb(j, s, carry):
                top, total = carry
                new = jnp.maximum(top, jnp.max(s, axis=0, keepdims=True) * log2e)
                e = jnp.exp2(s * log2e - new)
                e_ref[j] = e
                m_ref[j] = new
                total = total * jnp.exp2(top - new) + jnp.sum(e, axis=0, keepdims=True)
                return (new, total)

            carry = (jnp.full((1, rows), LOW, jnp.float32), jnp.zeros((1, rows), jnp.float32))
            carry = lax.fori_loop(first, last, lambda j, x: absorb(j, scores_of(j), x), carry)
            key_pos = lax.broadcasted_iota(jnp.int32, (toks, rows), 0)
            row_pos = tok0 + lax.broadcasted_iota(jnp.int32, (toks, rows), 1) // group
            top, total = absorb(
                0, jnp.where(key_pos <= row_pos, scores_of(0), LOW), carry
            )
            inverse = 1.0 / total

            def back(j, acc):
                prob = e_ref[j] * (jnp.exp2(m_ref[j] - top) * inverse)
                value_acc[j] += jnp.dot(
                    prob.astype(jnp.bfloat16), g_low, preferred_element_type=jnp.float32
                )
                dprob = lax.dot_general(
                    wide_ref[j],
                    g_wide,
                    (((1,), (1,)), ((), ())),
                    preferred_element_type=jnp.float32,
                )
                dscore = (prob * dprob).astype(jnp.bfloat16)
                key_acc[j] += jnp.dot(dscore, q, preferred_element_type=jnp.float32)
                return acc + lax.dot_general(
                    dscore,
                    keys_ref[j],
                    (((0,), (0,)), ((), ())),
                    preferred_element_type=jnp.float32,
                )

            acc = back(0, jnp.zeros((rows, dim), jnp.float32))
            acc = lax.fori_loop(first, last, back, acc)
            query_grad_ref[0, here] = (
                (acc * scale).reshape(chunk_tokens, group, dim).astype(query_grad_ref.dtype)
            )

        return 0

    lax.fori_loop(0, toks // chunk_tokens, chunk, 0)

    for j in range(slots):
        kv_grad_ref[j, 0, 0] = (key_acc[j] * scale).astype(kv_grad_ref.dtype)
        kv_grad_ref[j, 0, 1] = value_acc[j].astype(kv_grad_ref.dtype)


def attend(info, coef, query, grad, output, kvs, seq, first, kv_heads, whole):
    _, toks, heads, dim = query.shape
    slots = len(kvs)
    count = kvs[0].shape[0]
    group = heads // kv_heads
    chunk_tokens = min(CHUNK_TOKENS, toks)
    rows = chunk_tokens * group
    token_spec = pl.BlockSpec((1, toks, group, dim), lambda h, *_: (seq, 0, first + h, 0))
    kv_spec = pl.BlockSpec((1, 2, toks, dim), lambda h, *_: (h, 0, 0, 0))
    grad_spec = pl.BlockSpec((slots, 1, 2, toks, dim), lambda h, *_: (0, h, 0, 0, 0))
    operands = [info, coef, query, grad, output, *kvs]
    in_specs = [token_spec] * 3 + [kv_spec] * slots
    aliases = {}
    if whole is not None:
        aliases = {len(operands): 0}
        operands.append(whole)
        in_specs.append(pl.BlockSpec(memory_space=pl.ANY))
    flops = 5 * 2 * heads // kv_heads * count * toks * toks * slots * dim
    return pl.pallas_call(
        functools.partial(
            attend_kernel,
            slots=slots,
            scale=1.0 / math.sqrt(dim),
            seq=seq,
            chunk_tokens=chunk_tokens,
        ),
        out_shape=(
            jax.ShapeDtypeStruct(query.shape, query.dtype),
            jax.ShapeDtypeStruct((slots, count, 2, toks, dim), jnp.bfloat16),
        ),
        grid_spec=pltpu.PrefetchScalarGridSpec(
            num_scalar_prefetch=2,
            grid=(count,),
            in_specs=in_specs,
            out_specs=(token_spec, grad_spec),
            scratch_shapes=[
                pltpu.VMEM((slots, toks, rows), jnp.float32),
                pltpu.VMEM((slots, 1, rows), jnp.float32),
                pltpu.VMEM((slots, toks, dim), jnp.float32),
                pltpu.VMEM((slots, toks, dim), jnp.float32),
                pltpu.VMEM((slots, toks, dim), jnp.bfloat16),
                pltpu.VMEM((slots, toks, 2 * dim), jnp.bfloat16),
            ],
        ),
        input_output_aliases=aliases,
        cost_estimate=pl.CostEstimate(
            flops=flops,
            bytes_accessed=4 * 2 * toks * group * count * dim * 2,
            transcendentals=0,
        ),
        compiler_params=pltpu.CompilerParams(vmem_limit_bytes=48 * 1024 * 1024),
    )(*operands)


def spread(block, levels):
    across = lambda r, both: [
        (2 * z + x, 2 * z + 1 - x) for z in range(r, levels) for x in range(2 if both else 1)
    ]
    slots = [block, lax.ppermute(block, "seq", across(0, False))]
    for r in range(1, levels):
        up = [(2 * z + x, 2 * z + 2 + x) for z in range(r - 1, levels - 1) for x in range(2)]
        block = lax.ppermute(block, "seq", up)
        slots += [block, lax.ppermute(block, "seq", across(r, True))]
    return slots


def collect(parts, levels):
    total = None
    for r in range(levels - 1, -1, -1):
        pairs = [
            (2 * z + x, 2 * z + 1 - x)
            for z in range(r, levels)
            for x in (range(2) if r else range(1, 2))
        ]
        other = lax.ppermute(parts[2 * r + 1], "seq", pairs)
        mine = parts[2 * r].astype(jnp.float32) + other.astype(jnp.float32)
        if total is not None:
            down = [(2 * z + x, 2 * z - 2 + x) for z in range(r + 1, levels) for x in range(2)]
            mine = mine + lax.ppermute(total, "seq", down).astype(jnp.float32)
        total = mine.astype(parts.dtype)
    return total


def body(query, keys, values, output, out_grad, lengths, margins):
    place = lax.axis_index("seq")
    levels = lax.axis_size("seq") // 2
    seqs, toks, heads, dim = query.shape
    kv_heads = keys.shape[2]
    kv = jnp.stack([keys, values], axis=1).transpose(0, 3, 1, 2, 4)
    split = SPLIT
    step = kv_heads // split
    gathered = {
        (s, c): spread(kv[s, c : c + step], levels)
        for s in range(seqs)
        for c in range(0, kv_heads, step)
    }
    total = lax.psum(jnp.sum(lengths), "dp")
    mean_len = total.astype(jnp.float32) / (seqs * lax.axis_size("dp"))
    weight = jax.nn.sigmoid(-margins)
    signs = jnp.tile(jnp.array([-1.0, 1.0], jnp.float32), margins.shape[0])
    coef = jnp.repeat(weight, 2) * signs * 4.0 * mean_len / lengths.astype(jnp.float32)
    info = jnp.concatenate([jnp.stack([place, place % 2]), lengths]).astype(jnp.int32)
    query_grad = None
    parts = []
    for s in range(seqs):
        row = []
        for c in range(0, kv_heads, step):
            query_grad, kv_grad = attend(
                info, coef, query, out_grad, output, gathered[s, c], s, c, kv_heads, query_grad
            )
            row.append(collect(kv_grad, levels))
        parts.append(jnp.concatenate(row, axis=0) if split > 1 else row[0])
    grads = jnp.stack(parts)
    key_grad = grads[:, :, 0].transpose(0, 2, 1, 3)
    value_grad = grads[:, :, 1].transpose(0, 2, 1, 3)
    return (query_grad, key_grad, value_grad)


def solution(mesh):
    tokens = P("dp", "seq", None, None)
    return jax.shard_map(
        body,
        mesh=mesh,
        in_specs=(tokens,) * 5 + (P("dp"), P("dp")),
        out_specs=(tokens,) * 3,
        check_vma=False,
    )
```

```python
import functools
import math

import jax
import jax.numpy as jnp
from jax import lax
from jax.experimental import pallas as pl
from jax.experimental.pallas import tpu as pltpu
from jax.sharding import PartitionSpec as P

CHUNK_TOKENS = 32
SPLIT = 2
LOW = -1e30


def attend_kernel(
    info,
    coef,
    query_ref,
    grad_ref,
    output_ref,
    kv_ref,
    *rest,
    scale,
    seq,
    chunk_tokens,
):
    query_grad_ref, kv_grad_ref, e_ref, dp_ref, key_acc, value_acc, keys_ref, wide_ref = rest[-8:]
    toks, group, dim = query_ref.shape[1:]
    levels = kv_ref.shape[0] // 2
    rows = chunk_tokens * group
    place = info[0]
    side = info[1]
    length = info[2 + seq]
    factor_live = coef[seq]
    base = place * toks
    last = place // 2 + 1
    log2e = scale * math.log2(math.e)

    lane = lax.broadcasted_iota(jnp.int32, (2 * toks, dim), 1)
    ones = jnp.where(lane < 3, 1.0, 0.0).astype(jnp.bfloat16)
    for r in range(levels):
        level = jnp.maximum(place // 2 - r, 0)
        key_acc[r] = jnp.zeros((2 * toks, dim), jnp.float32)
        value_acc[r] = jnp.zeros((2 * toks, dim), jnp.float32)
        for w, owner in enumerate((2 * level + side, 2 * level + 1 - side)):
            keys_ref[r, w * toks : (w + 1) * toks] = kv_ref[owner, 0, 0]
            wide_ref[r, w * toks : (w + 1) * toks, :dim] = kv_ref[owner, 0, 1]
        wide_ref[r, :, dim:] = ones

    def chunk(c, _):
        tok0 = pl.multiple_of(c * chunk_tokens, chunk_tokens)
        here = pl.ds(tok0, chunk_tokens)

        @pl.when(base + tok0 >= length)
        def _():
            query_grad_ref[0, here] = jnp.zeros((chunk_tokens, group, dim), query_grad_ref.dtype)

        @pl.when(base + tok0 < length)
        def _():
            q = (
                query_ref[0, here].astype(jnp.float32).reshape(rows, dim).astype(jnp.bfloat16)
            )
            position = (
                base + tok0 + lax.broadcasted_iota(jnp.int32, (chunk_tokens, group, dim), 0)
            )
            factor = jnp.where(position < length, factor_live, 0.0)
            g = (grad_ref[0, here].astype(jnp.float32) * factor).reshape(rows, dim)
            g_low = g.astype(jnp.bfloat16)
            o = output_ref[0, here].astype(jnp.float32).reshape(rows, dim)
            delta = jnp.sum(g_low.astype(jnp.float32) * o, axis=-1, keepdims=True)
            high = delta.astype(jnp.bfloat16).astype(jnp.float32)
            middle = (delta - high).astype(jnp.bfloat16).astype(jnp.float32)
            low = delta - high - middle
            row_lane = lax.broadcasted_iota(jnp.int32, (rows, dim), 1)
            extra = jnp.where(
                row_lane == 0,
                -high,
                jnp.where(row_lane == 1, -middle, jnp.where(row_lane == 2, -low, 0.0)),
            ).astype(jnp.bfloat16)
            g_wide = jnp.concatenate([g_low, extra], axis=1)

            def scores_of(j):
                return lax.dot_general(
                    keys_ref[j],
                    q,
                    (((1,), (1,)), ((), ())),
                    preferred_element_type=jnp.float32,
                )

            def keep(r, s, top):
                e_ref[r] = s
                return jnp.maximum(top, jnp.max(s.reshape(-1, 8, rows), axis=0))

            key_row = lax.broadcasted_iota(jnp.int32, (2 * toks, rows), 0)
            row_pos = tok0 + lax.broadcasted_iota(jnp.int32, (2 * toks, rows), 1) // group
            seen = (key_row <= row_pos) | (key_row >= 2 * toks - toks * side)
            top = keep(
                0, jnp.where(seen, scores_of(0), LOW), jnp.full((8, rows), LOW, jnp.float32)
            )
            top = lax.fori_loop(1, last, lambda r, x: keep(r, scores_of(r), x), top)
            top = jnp.max(top, axis=0, keepdims=True) * log2e

            def weigh(r, total):
                e = jnp.exp2(e_ref[r] * log2e - top)
                e_ref[r] = e
                dp_ref[r] = lax.dot_general(
                    wide_ref[r],
                    g_wide,
                    (((1,), (1,)), ((), ())),
                    preferred_element_type=jnp.float32,
                )
                return total + jnp.sum(e.reshape(-1, 8, rows), axis=0)

            total = lax.fori_loop(0, last, weigh, jnp.zeros((8, rows), jnp.float32))
            inverse = 1.0 / jnp.sum(total, axis=0, keepdims=True)

            def back(r, acc):
                prob = e_ref[r] * inverse
                dscore = (prob * dp_ref[r]).astype(jnp.bfloat16)
                value_acc[r] += jnp.dot(
                    prob.astype(jnp.bfloat16), g_low, preferred_element_type=jnp.float32
                )
                key_acc[r] += jnp.dot(dscore, q, preferred_element_type=jnp.float32)
                return acc + lax.dot_general(
                    dscore,
                    keys_ref[r],
                    (((0,), (0,)), ((), ())),
                    preferred_element_type=jnp.float32,
                )

            acc = lax.fori_loop(0, last, back, jnp.zeros((rows, dim), jnp.float32))
            query_grad_ref[0, here] = (
                (acc * scale).reshape(chunk_tokens, group, dim).astype(query_grad_ref.dtype)
            )

        return 0

    lax.fori_loop(0, toks // chunk_tokens, chunk, 0)

    for r in range(levels):
        for w in range(2):
            half = slice(w * toks, (w + 1) * toks)
            kv_grad_ref[2 * r + w, 0, 0] = (key_acc[r, half] * scale).astype(kv_grad_ref.dtype)
            kv_grad_ref[2 * r + w, 0, 1] = value_acc[r, half].astype(kv_grad_ref.dtype)


def attend(info, coef, query, grad, output, kv, seq, first, kv_heads, whole):
    _, toks, heads, dim = query.shape
    slots, count = kv.shape[:2]
    levels = slots // 2
    group = heads // kv_heads
    chunk_tokens = min(CHUNK_TOKENS, toks)
    rows = chunk_tokens * group
    token_spec = pl.BlockSpec((1, toks, group, dim), lambda h, *_: (seq, 0, first + h, 0))
    kv_spec = pl.BlockSpec((slots, 1, 2, toks, dim), lambda h, *_: (0, h, 0, 0, 0))
    grad_spec = pl.BlockSpec((slots, 1, 2, toks, dim), lambda h, *_: (0, h, 0, 0, 0))
    operands = [info, coef, query, grad, output, kv]
    in_specs = [token_spec] * 3 + [kv_spec]
    aliases = {}
    if whole is not None:
        aliases = {len(operands): 0}
        operands.append(whole)
        in_specs.append(pl.BlockSpec(memory_space=pl.ANY))
    flops = 5 * 2 * heads // kv_heads * count * toks * toks * slots * dim
    return pl.pallas_call(
        functools.partial(
            attend_kernel,
            scale=1.0 / math.sqrt(dim),
            seq=seq,
            chunk_tokens=chunk_tokens,
        ),
        out_shape=(
            jax.ShapeDtypeStruct(query.shape, query.dtype),
            jax.ShapeDtypeStruct((slots, count, 2, toks, dim), jnp.bfloat16),
        ),
        grid_spec=pltpu.PrefetchScalarGridSpec(
            num_scalar_prefetch=2,
            grid=(count,),
            in_specs=in_specs,
            out_specs=(token_spec, grad_spec),
            scratch_shapes=[
                pltpu.VMEM((levels, 2 * toks, rows), jnp.float32),
                pltpu.VMEM((levels, 2 * toks, rows), jnp.float32),
                pltpu.VMEM((levels, 2 * toks, dim), jnp.float32),
                pltpu.VMEM((levels, 2 * toks, dim), jnp.float32),
                pltpu.VMEM((levels, 2 * toks, dim), jnp.bfloat16),
                pltpu.VMEM((levels, 2 * toks, 2 * dim), jnp.bfloat16),
            ],
        ),
        input_output_aliases=aliases,
        cost_estimate=pl.CostEstimate(
            flops=flops,
            bytes_accessed=4 * 2 * toks * group * count * dim * 2,
            transcendentals=0,
        ),
        compiler_params=pltpu.CompilerParams(vmem_limit_bytes=48 * 1024 * 1024),
    )(*operands)


def collect(parts, levels):
    total = None
    for r in range(levels - 1, -1, -1):
        pairs = [
            (2 * z + x, 2 * z + 1 - x)
            for z in range(r, levels)
            for x in (range(2) if r else range(1, 2))
        ]
        other = lax.ppermute(parts[2 * r + 1], "seq", pairs)
        mine = parts[2 * r].astype(jnp.float32) + other.astype(jnp.float32)
        if total is not None:
            down = [(2 * z + x, 2 * z - 2 + x) for z in range(r + 1, levels) for x in range(2)]
            mine = mine + lax.ppermute(total, "seq", down).astype(jnp.float32)
        total = mine.astype(parts.dtype)
    return total


def body(query, keys, values, output, out_grad, lengths, margins):
    place = lax.axis_index("seq")
    levels = lax.axis_size("seq") // 2
    seqs, toks, heads, dim = query.shape
    kv_heads = keys.shape[2]
    kv = jnp.stack([keys, values], axis=1).transpose(0, 3, 1, 2, 4)
    split = SPLIT
    step = kv_heads // split
    gathered = {
        (s, c): lax.all_gather(kv[s, c : c + step], "seq", axis=0, tiled=False)
        for s in range(seqs)
        for c in range(0, kv_heads, step)
    }
    total = lax.psum(jnp.sum(lengths), "dp")
    mean_len = total.astype(jnp.float32) / (seqs * lax.axis_size("dp"))
    weight = jax.nn.sigmoid(-margins)
    signs = jnp.tile(jnp.array([-1.0, 1.0], jnp.float32), margins.shape[0])
    coef = jnp.repeat(weight, 2) * signs * 4.0 * mean_len / lengths.astype(jnp.float32)
    info = jnp.concatenate([jnp.stack([place, place % 2]), lengths]).astype(jnp.int32)
    query_grad = None
    parts = []
    for s in range(seqs):
        row = []
        for c in range(0, kv_heads, step):
            query_grad, kv_grad = attend(
                info, coef, query, out_grad, output, gathered[s, c], s, c, kv_heads, query_grad
            )
            row.append(collect(kv_grad, levels))
        parts.append(jnp.concatenate(row, axis=0) if split > 1 else row[0])
    grads = jnp.stack(parts)
    key_grad = grads[:, :, 0].transpose(0, 2, 1, 3)
    value_grad = grads[:, :, 1].transpose(0, 2, 1, 3)
    return (query_grad, key_grad, value_grad)


def solution(mesh):
    tokens = P("dp", "seq", None, None)
    return jax.shard_map(
        body,
        mesh=mesh,
        in_specs=(tokens,) * 5 + (P("dp"), P("dp")),
        out_specs=(tokens,) * 3,
        check_vma=False,
    )
```

```python
import functools
import math

import jax
import jax.numpy as jnp
from jax import lax
from jax.experimental import pallas as pl
from jax.experimental.pallas import tpu as pltpu
from jax.sharding import PartitionSpec as P

CHUNK_TOKENS = 64
LOW = -1e30


def attend_kernel(
    info,
    coef,
    query_ref,
    grad_ref,
    output_ref,
    kv_ref,
    *rest,
    scale,
    seq,
    chunk_tokens,
):
    query_grad_ref, mine_ref, other_ref, *scratch = rest[-10:]
    s_ref, e_ref, dp_ref, key_acc, value_acc, keys_ref, wide_ref = scratch
    toks, group, dim = query_ref.shape[1:]
    levels = kv_ref.shape[0] // 2
    rows = chunk_tokens * group
    place = info[0]
    side = info[1]
    length = info[2 + seq]
    factor_live = coef[seq]
    base = place * toks
    last = place // 2 + 1
    log2e = scale * math.log2(math.e)

    lane = lax.broadcasted_iota(jnp.int32, (2 * toks, dim), 1)
    ones = jnp.where(lane < 3, 1.0, 0.0).astype(jnp.bfloat16)
    for r in range(levels):
        level = jnp.maximum(place // 2 - r, 0)
        key_acc[r] = jnp.zeros((2 * toks, dim), jnp.float32)
        value_acc[r] = jnp.zeros((2 * toks, dim), jnp.float32)
        for w, owner in enumerate((2 * level + side, 2 * level + 1 - side)):
            keys_ref[r, w * toks : (w + 1) * toks] = kv_ref[owner, 0, 0]
            wide_ref[r, w * toks : (w + 1) * toks, :dim] = kv_ref[owner, 0, 1]
        wide_ref[r, :, dim:] = ones

    def chunk(c, _):
        tok0 = pl.multiple_of(c * chunk_tokens, chunk_tokens)
        here = pl.ds(tok0, chunk_tokens)

        @pl.when(base + tok0 >= length)
        def _():
            query_grad_ref[0, here] = jnp.zeros((chunk_tokens, group, dim), query_grad_ref.dtype)

        @pl.when(base + tok0 < length)
        def _():
            q = (
                query_ref[0, here].astype(jnp.float32).reshape(rows, dim).astype(jnp.bfloat16)
            )
            position = (
                base + tok0 + lax.broadcasted_iota(jnp.int32, (chunk_tokens, group, dim), 0)
            )
            factor = jnp.where(position < length, factor_live, 0.0)
            g = (grad_ref[0, here].astype(jnp.float32) * factor).reshape(rows, dim)
            g_low = g.astype(jnp.bfloat16)
            o = output_ref[0, here].astype(jnp.float32).reshape(rows, dim)
            delta = jnp.sum(g_low.astype(jnp.float32) * o, axis=-1, keepdims=True)
            high = delta.astype(jnp.bfloat16).astype(jnp.float32)
            middle = (delta - high).astype(jnp.bfloat16).astype(jnp.float32)
            low = delta - high - middle
            row_lane = lax.broadcasted_iota(jnp.int32, (rows, dim), 1)
            extra = jnp.where(
                row_lane == 0,
                -high,
                jnp.where(row_lane == 1, -middle, jnp.where(row_lane == 2, -low, 0.0)),
            ).astype(jnp.bfloat16)
            g_wide = jnp.concatenate([g_low, extra], axis=1)

            def scores_of(j):
                return lax.dot_general(
                    keys_ref[j],
                    q,
                    (((1,), (1,)), ((), ())),
                    preferred_element_type=jnp.float32,
                )

            def keep(r, s, top):
                s_ref[r] = s
                return jnp.maximum(top, jnp.max(s.reshape(-1, 8, rows), axis=0))

            key_row = lax.broadcasted_iota(jnp.int32, (2 * toks, rows), 0)
            row_pos = tok0 + lax.broadcasted_iota(jnp.int32, (2 * toks, rows), 1) // group
            seen = (key_row <= row_pos) | (key_row >= 2 * toks - toks * side)
            top = keep(
                0, jnp.where(seen, scores_of(0), LOW), jnp.full((8, rows), LOW, jnp.float32)
            )
            top = lax.fori_loop(1, last, lambda r, x: keep(r, scores_of(r), x), top)
            top = jnp.max(top, axis=0, keepdims=True) * log2e

            def weigh(r, total):
                e = jnp.exp2(s_ref[r] * log2e - top)
                e_ref[r] = e.astype(jnp.bfloat16)
                dp_ref[r] = lax.dot_general(
                    wide_ref[r],
                    g_wide,
                    (((1,), (1,)), ((), ())),
                    preferred_element_type=jnp.float32,
                ).astype(jnp.bfloat16)
                return total + jnp.sum(e.reshape(-1, 8, rows), axis=0)

            total = lax.fori_loop(0, last, weigh, jnp.zeros((8, rows), jnp.float32))
            inverse = 1.0 / jnp.sum(total, axis=0, keepdims=True)
            column = jnp.transpose(jnp.broadcast_to(inverse, (dim, rows)))
            q_norm = (q.astype(jnp.float32) * column).astype(jnp.bfloat16)
            g_norm = (g_low.astype(jnp.float32) * column).astype(jnp.bfloat16)

            def back(r, acc):
                e = e_ref[r]
                dscore = e * dp_ref[r]
                value_acc[r] += jnp.dot(e, g_norm, preferred_element_type=jnp.float32)
                key_acc[r] += jnp.dot(dscore, q_norm, preferred_element_type=jnp.float32)
                return acc + lax.dot_general(
                    dscore,
                    keys_ref[r],
                    (((0,), (0,)), ((), ())),
                    preferred_element_type=jnp.float32,
                )

            acc = lax.fori_loop(0, last, back, jnp.zeros((rows, dim), jnp.float32))
            acc = acc * column
            query_grad_ref[0, here] = (
                (acc * scale).reshape(chunk_tokens, group, dim).astype(query_grad_ref.dtype)
            )

        return 0

    lax.fori_loop(0, toks // chunk_tokens, chunk, 0)

    for r in range(levels):
        for w, ref in enumerate((mine_ref, other_ref)):
            half = slice(w * toks, (w + 1) * toks)
            ref[r, 0, 0] = (key_acc[r, half] * scale).astype(ref.dtype)
            ref[r, 0, 1] = value_acc[r, half].astype(ref.dtype)


def attend(info, coef, query, grad, output, kv, seq, first, kv_heads, whole):
    _, toks, heads, dim = query.shape
    slots, count = kv.shape[:2]
    levels = slots // 2
    group = heads // kv_heads
    chunk_tokens = min(CHUNK_TOKENS, toks)
    rows = chunk_tokens * group
    token_spec = pl.BlockSpec((1, toks, group, dim), lambda h, *_: (seq, 0, first + h, 0))
    kv_spec = pl.BlockSpec((slots, 1, 2, toks, dim), lambda h, *_: (0, h, 0, 0, 0))
    grad_spec = pl.BlockSpec((levels, 1, 2, toks, dim), lambda h, *_: (0, h, 0, 0, 0))
    operands = [info, coef, query, grad, output, kv]
    in_specs = [token_spec] * 3 + [kv_spec]
    aliases = {}
    if whole is not None:
        aliases = {len(operands): 0}
        operands.append(whole)
        in_specs.append(pl.BlockSpec(memory_space=pl.ANY))
    flops = 5 * 2 * heads // kv_heads * count * toks * toks * slots * dim
    return pl.pallas_call(
        functools.partial(
            attend_kernel,
            scale=1.0 / math.sqrt(dim),
            seq=seq,
            chunk_tokens=chunk_tokens,
        ),
        out_shape=(
            jax.ShapeDtypeStruct(query.shape, query.dtype),
            jax.ShapeDtypeStruct((levels, count, 2, toks, dim), jnp.bfloat16),
            jax.ShapeDtypeStruct((levels, count, 2, toks, dim), jnp.bfloat16),
        ),
        grid_spec=pltpu.PrefetchScalarGridSpec(
            num_scalar_prefetch=2,
            grid=(count,),
            in_specs=in_specs,
            out_specs=(token_spec, grad_spec, grad_spec),
            scratch_shapes=[
                pltpu.VMEM((levels, 2 * toks, rows), jnp.float32),
                pltpu.VMEM((levels, 2 * toks, rows), jnp.bfloat16),
                pltpu.VMEM((levels, 2 * toks, rows), jnp.bfloat16),
                pltpu.VMEM((levels, 2 * toks, dim), jnp.float32),
                pltpu.VMEM((levels, 2 * toks, dim), jnp.float32),
                pltpu.VMEM((levels, 2 * toks, dim), jnp.bfloat16),
                pltpu.VMEM((levels, 2 * toks, 2 * dim), jnp.bfloat16),
            ],
        ),
        input_output_aliases=aliases,
        cost_estimate=pl.CostEstimate(
            flops=flops,
            bytes_accessed=4 * 2 * toks * group * count * dim * 2,
            transcendentals=0,
        ),
        compiler_params=pltpu.CompilerParams(vmem_limit_bytes=48 * 1024 * 1024),
    )(*operands)


def collect(mine, other, levels):
    swap = [(i, i + 1 - 2 * (i % 2)) for i in range(2 * levels)]
    other = lax.ppermute(other, "seq", swap).astype(jnp.float32)
    column = mine.astype(jnp.float32) + other
    total = column[0]
    low = column.astype(mine.dtype)
    for r in range(1, levels):
        down = [(i, i - 2 * r) for i in range(2 * r, 2 * levels)]
        total = total + lax.ppermute(low[r], "seq", down).astype(jnp.float32)
    return total.astype(mine.dtype)


def body(query, keys, values, output, out_grad, lengths, margins):
    place = lax.axis_index("seq")
    levels = lax.axis_size("seq") // 2
    seqs, toks, heads, dim = query.shape
    kv_heads = keys.shape[2]
    kv = jnp.stack([keys, values], axis=1).transpose(0, 3, 1, 2, 4)
    quarter = max(1, kv_heads // 4)
    sizes = [quarter, quarter, kv_heads - 2 * quarter]
    cuts = {}
    for s in range(seqs):
        order = sizes if s < seqs - 1 else sizes[::-1]
        cuts[s] = [(sum(order[:i]), n) for i, n in enumerate(order) if n]
    gathered = {
        (s, c): lax.all_gather(kv[s, c : c + n], "seq", axis=0, tiled=False)
        for s in range(seqs)
        for c, n in cuts[s]
    }
    total = lax.psum(jnp.sum(lengths), "dp")
    mean_len = total.astype(jnp.float32) / (seqs * lax.axis_size("dp"))
    weight = jax.nn.sigmoid(-margins)
    signs = jnp.tile(jnp.array([-1.0, 1.0], jnp.float32), margins.shape[0])
    coef = jnp.repeat(weight, 2) * signs * 4.0 * mean_len / lengths.astype(jnp.float32)
    info = jnp.concatenate([jnp.stack([place, place % 2]), lengths]).astype(jnp.int32)
    query_grad = None
    parts = []
    for s in range(seqs):
        row = []
        for c, _ in cuts[s]:
            query_grad, mine, other = attend(
                info, coef, query, out_grad, output, gathered[s, c], s, c, kv_heads, query_grad
            )
            row.append(collect(mine, other, levels))
        parts.append(jnp.concatenate(row, axis=0))
    grads = jnp.stack(parts)
    key_grad = grads[:, :, 0].transpose(0, 2, 1, 3)
    value_grad = grads[:, :, 1].transpose(0, 2, 1, 3)
    return (query_grad, key_grad, value_grad)


def solution(mesh):
    tokens = P("dp", "seq", None, None)
    return jax.shard_map(
        body,
        mesh=mesh,
        in_specs=(tokens,) * 5 + (P("dp"), P("dp")),
        out_specs=(tokens,) * 3,
        check_vma=False,
    )
```

```python
import functools
import math

import jax
import jax.numpy as jnp
from jax import lax
from jax.experimental import pallas as pl
from jax.experimental.pallas import tpu as pltpu
from jax.sharding import PartitionSpec as P

CHUNK_TOKENS = 64
LOW = -1e30


def attend_kernel(
    info,
    coef,
    query_ref,
    grad_ref,
    output_ref,
    kv_ref,
    *rest,
    scale,
    seq,
    chunk_tokens,
):
    query_grad_ref, mine_ref, other_ref, *scratch = rest[-10:]
    s_ref, e_ref, dp_ref, key_acc, value_acc, keys_ref, wide_ref = scratch
    toks, group, dim = query_ref.shape[1:]
    levels = kv_ref.shape[0] // 2
    rows = chunk_tokens * group
    place = info[0]
    side = info[1]
    length = info[2 + seq]
    factor_live = coef[seq]
    base = place * toks
    last = place // 2 + 1
    log2e = scale * math.log2(math.e)

    lane = lax.broadcasted_iota(jnp.int32, (2 * toks, dim), 1)
    ones = jnp.where(lane < 3, 1.0, 0.0).astype(jnp.bfloat16)
    for r in range(levels):
        level = jnp.maximum(place // 2 - r, 0)
        key_acc[r] = jnp.zeros((2 * toks, dim), jnp.float32)
        value_acc[r] = jnp.zeros((2 * toks, dim), jnp.float32)
        for w, owner in enumerate((2 * level + side, 2 * level + 1 - side)):
            keys_ref[r, w * toks : (w + 1) * toks] = kv_ref[owner, 0, 0]
            wide_ref[r, w * toks : (w + 1) * toks, :dim] = kv_ref[owner, 0, 1]
        wide_ref[r, :, dim:] = ones

    def chunk(c, _):
        tok0 = pl.multiple_of(c * chunk_tokens, chunk_tokens)
        here = pl.ds(tok0, chunk_tokens)

        @pl.when(base + tok0 >= length)
        def _():
            query_grad_ref[0, here] = jnp.zeros((chunk_tokens, group, dim), query_grad_ref.dtype)

        @pl.when(base + tok0 < length)
        def _():
            q = (
                query_ref[0, here].astype(jnp.float32).reshape(rows, dim).astype(jnp.bfloat16)
            )
            position = (
                base + tok0 + lax.broadcasted_iota(jnp.int32, (chunk_tokens, group, dim), 0)
            )
            factor = jnp.where(position < length, factor_live, 0.0)
            g = (grad_ref[0, here].astype(jnp.float32) * factor).reshape(rows, dim)
            g_low = g.astype(jnp.bfloat16)
            o = output_ref[0, here].astype(jnp.float32).reshape(rows, dim)
            delta = jnp.sum(g_low.astype(jnp.float32) * o, axis=-1, keepdims=True)
            high = delta.astype(jnp.bfloat16).astype(jnp.float32)
            middle = (delta - high).astype(jnp.bfloat16).astype(jnp.float32)
            low = delta - high - middle
            row_lane = lax.broadcasted_iota(jnp.int32, (rows, dim), 1)
            extra = jnp.where(
                row_lane == 0,
                -high,
                jnp.where(row_lane == 1, -middle, jnp.where(row_lane == 2, -low, 0.0)),
            ).astype(jnp.bfloat16)
            g_wide = jnp.concatenate([g_low, extra], axis=1)

            def scores_of(j):
                return lax.dot_general(
                    keys_ref[j],
                    q,
                    (((1,), (1,)), ((), ())),
                    preferred_element_type=jnp.float32,
                )

            def keep(r, s, top):
                s_ref[r] = s
                return jnp.maximum(top, jnp.max(s.reshape(-1, 8, rows), axis=0))

            key_row = lax.broadcasted_iota(jnp.int32, (2 * toks, rows), 0)
            row_pos = tok0 + lax.broadcasted_iota(jnp.int32, (2 * toks, rows), 1) // group
            seen = (key_row <= row_pos) | (key_row >= 2 * toks - toks * side)
            top = keep(
                0, jnp.where(seen, scores_of(0), LOW), jnp.full((8, rows), LOW, jnp.float32)
            )
            top = lax.fori_loop(1, last, lambda r, x: keep(r, scores_of(r), x), top)
            top = jnp.max(top, axis=0, keepdims=True) * log2e

            def weigh(r, total):
                e = jnp.exp2(s_ref[r] * log2e - top)
                e_ref[r] = e.astype(jnp.bfloat16)
                dp_ref[r] = lax.dot_general(
                    wide_ref[r],
                    g_wide,
                    (((1,), (1,)), ((), ())),
                    preferred_element_type=jnp.float32,
                ).astype(jnp.bfloat16)
                return total + jnp.sum(e.reshape(-1, 8, rows), axis=0)

            total = lax.fori_loop(0, last, weigh, jnp.zeros((8, rows), jnp.float32))
            inverse = 1.0 / jnp.sum(total, axis=0, keepdims=True)
            column = jnp.transpose(jnp.broadcast_to(inverse, (dim, rows)))
            q_norm = (q.astype(jnp.float32) * column).astype(jnp.bfloat16)
            g_norm = (g_low.astype(jnp.float32) * column).astype(jnp.bfloat16)

            def back(r, acc):
                e = e_ref[r]
                dscore = e * dp_ref[r]
                value_acc[r] += jnp.dot(e, g_norm, preferred_element_type=jnp.float32)
                key_acc[r] += jnp.dot(dscore, q_norm, preferred_element_type=jnp.float32)
                return acc + lax.dot_general(
                    dscore,
                    keys_ref[r],
                    (((0,), (0,)), ((), ())),
                    preferred_element_type=jnp.float32,
                )

            acc = lax.fori_loop(0, last, back, jnp.zeros((rows, dim), jnp.float32))
            acc = acc * column
            query_grad_ref[0, here] = (
                (acc * scale).reshape(chunk_tokens, group, dim).astype(query_grad_ref.dtype)
            )

        return 0

    lax.fori_loop(0, toks // chunk_tokens, chunk, 0)

    for r in range(levels):
        for w, ref in enumerate((mine_ref, other_ref)):
            half = slice(w * toks, (w + 1) * toks)
            ref[r, 0, 0] = (key_acc[r, half] * scale).astype(ref.dtype)
            ref[r, 0, 1] = value_acc[r, half].astype(ref.dtype)


def attend(info, coef, query, grad, output, kv, skip, count, seq, first, kv_heads, whole):
    _, toks, heads, dim = query.shape
    slots = kv.shape[0]
    levels = slots // 2
    group = heads // kv_heads
    chunk_tokens = min(CHUNK_TOKENS, toks)
    rows = chunk_tokens * group
    token_spec = pl.BlockSpec((1, toks, group, dim), lambda h, *_: (seq, 0, first + h, 0))
    kv_spec = pl.BlockSpec((slots, 1, 2, toks, dim), lambda h, *_: (0, skip + h, 0, 0, 0))
    grad_spec = pl.BlockSpec((levels, 1, 2, toks, dim), lambda h, *_: (0, h, 0, 0, 0))
    operands = [info, coef, query, grad, output, kv]
    in_specs = [token_spec] * 3 + [kv_spec]
    aliases = {}
    if whole is not None:
        aliases = {len(operands): 0}
        operands.append(whole)
        in_specs.append(pl.BlockSpec(memory_space=pl.ANY))
    flops = 5 * 2 * heads // kv_heads * count * toks * toks * slots * dim
    return pl.pallas_call(
        functools.partial(
            attend_kernel,
            scale=1.0 / math.sqrt(dim),
            seq=seq,
            chunk_tokens=chunk_tokens,
        ),
        out_shape=(
            jax.ShapeDtypeStruct(query.shape, query.dtype),
            jax.ShapeDtypeStruct((levels, count, 2, toks, dim), jnp.bfloat16),
            jax.ShapeDtypeStruct((levels, count, 2, toks, dim), jnp.bfloat16),
        ),
        grid_spec=pltpu.PrefetchScalarGridSpec(
            num_scalar_prefetch=2,
            grid=(count,),
            in_specs=in_specs,
            out_specs=(token_spec, grad_spec, grad_spec),
            scratch_shapes=[
                pltpu.VMEM((levels, 2 * toks, rows), jnp.float32),
                pltpu.VMEM((levels, 2 * toks, rows), jnp.bfloat16),
                pltpu.VMEM((levels, 2 * toks, rows), jnp.bfloat16),
                pltpu.VMEM((levels, 2 * toks, dim), jnp.float32),
                pltpu.VMEM((levels, 2 * toks, dim), jnp.float32),
                pltpu.VMEM((levels, 2 * toks, dim), jnp.bfloat16),
                pltpu.VMEM((levels, 2 * toks, 2 * dim), jnp.bfloat16),
            ],
        ),
        input_output_aliases=aliases,
        cost_estimate=pl.CostEstimate(
            flops=flops,
            bytes_accessed=4 * 2 * toks * group * count * dim * 2,
            transcendentals=0,
        ),
        compiler_params=pltpu.CompilerParams(vmem_limit_bytes=48 * 1024 * 1024),
    )(*operands)


def collect(mine, other, levels):
    swap = [(i, i + 1 - 2 * (i % 2)) for i in range(2 * levels)]
    other = lax.ppermute(other, "seq", swap).astype(jnp.float32)
    column = mine.astype(jnp.float32) + other
    total = column[0]
    low = column.astype(mine.dtype)
    for r in range(1, levels):
        down = [(i, i - 2 * r) for i in range(2 * r, 2 * levels)]
        total = total + lax.ppermute(low[r], "seq", down).astype(jnp.float32)
    return total.astype(mine.dtype)


def body(query, keys, values, output, out_grad, lengths, margins):
    place = lax.axis_index("seq")
    levels = lax.axis_size("seq") // 2
    seqs, toks, heads, dim = query.shape
    kv_heads = keys.shape[2]
    kv = jnp.stack([keys, values], axis=1).transpose(0, 3, 1, 2, 4)
    half = max(1, kv_heads // 2)
    gathered = {}
    for s in range(seqs):
        width = half if s == 0 else kv_heads
        for c in range(0, kv_heads, width):
            whole = lax.all_gather(kv[s, c : c + width], "seq", axis=0, tiled=False)
            gathered.update({(s, c + k): (whole, k) for k in range(0, width, half)})
    total = lax.psum(jnp.sum(lengths), "dp")
    mean_len = total.astype(jnp.float32) / (seqs * lax.axis_size("dp"))
    weight = jax.nn.sigmoid(-margins)
    signs = jnp.tile(jnp.array([-1.0, 1.0], jnp.float32), margins.shape[0])
    coef = jnp.repeat(weight, 2) * signs * 4.0 * mean_len / lengths.astype(jnp.float32)
    info = jnp.concatenate([jnp.stack([place, place % 2]), lengths]).astype(jnp.int32)
    query_grad = None
    parts = []
    for s in range(seqs):
        row = []
        for c in range(0, kv_heads, half):
            kv_all, skip = gathered[s, c]
            query_grad, mine, other = attend(
                info, coef, query, out_grad, output, kv_all, skip, half, s, c, kv_heads, query_grad
            )
            row.append(collect(mine, other, levels))
        parts.append(jnp.concatenate(row, axis=0))
    grads = jnp.stack(parts)
    key_grad = grads[:, :, 0].transpose(0, 2, 1, 3)
    value_grad = grads[:, :, 1].transpose(0, 2, 1, 3)
    return (query_grad, key_grad, value_grad)


def solution(mesh):
    tokens = P("dp", "seq", None, None)
    return jax.shard_map(
        body,
        mesh=mesh,
        in_specs=(tokens,) * 5 + (P("dp"), P("dp")),
        out_specs=(tokens,) * 3,
        check_vma=False,
    )
```
